32 devices in a mesh: group: 2 (over x), loop: 16 (over z, y, core).
Axes of the slice: x: 2, y: 2, z: 4, core: 2. Of those that a mesh axis runs over, the one named last changes fastest.
Arguments:
- users: float32 [8192, 512], P(('group', 'loop')), parts along dimension 0, may hold values from -1.3 to 1.3
- items: bfloat16 [4096, 512], P(('group', 'loop')), parts along dimension 0, may hold values from -1.296875 to 1.296875
- tile_blocks: int32 [32, 8], P(('group', 'loop')), parts along dimension 0, may hold values from 0 to 15, as said below
- tile_count: int32 [32], P(('group', 'loop')), parts along dimension 0, may hold values from 1 to 8, as said below
- labels: int32 [8192, 1024], P(('group', 'loop')), parts along dimension 0, may hold values 0 or 1
Outputs:
- new_users: float32 [8192, 512], P(('group', 'loop')), parts along dimension 0
The draws below stay inside these ranges and needn't reach their ends.
There are 2 independent parts, one for each index of `group`. The reference program is written for one: setup_inputs(seed, part) draws one part's arguments, and reference() takes and returns one part's arrays. A program takes and returns all parts, laid end to end along the dimension named above; each array names one. Nothing has to cross between parts.
Inputs may be any that keep to these rules, and one draw needn't show every extreme that they name: `tile_blocks`: in each row the entries are distinct item blocks; only the first tile_count of them are used. `tile_count`: some user block has all 8 tiles live.
All inputs are finite; a program needn't handle non-finite values. No bound on the sum of `labels` on one device may be relied on, other than what follows from the above.
Results may differ from the reference program's by a relative error of at most 0.0003.
Values may be sent and summed in bfloat16 or wider, within the bound.
A program may use at most 64 MiB of HBM per device.

```python
import jax
import jax.numpy as jnp
from jax import lax

K = 512
USR_DEV = 256
ITEM_DEV = 128
SLOTS = 8
NU = 4096
NI = 2048
N_LOOP = 16


def draw_tile_blocks(key, part):
    row_keys = jax.random.split(jax.random.fold_in(key, 7), N_LOOP)
    shuffled = jax.vmap(lambda row_key: jax.random.permutation(row_key, N_LOOP))(row_keys)
    return shuffled[:, :SLOTS].astype(jnp.int32)


def draw_tile_count(key, part):
    shifts = jax.random.randint(jax.random.fold_in(key, 11), (N_LOOP,), 0, 4)
    counts_drawn = jnp.floor_divide(SLOTS, jnp.left_shift(1, shifts))
    busiest = jax.random.randint(jax.random.fold_in(key, 13), (), 0, N_LOOP)
    positions = jnp.arange(N_LOOP)
    return jnp.where(positions == busiest, SLOTS, counts_drawn).astype(jnp.int32)


def plant(values, rng, least, largest):
    longest = values.shape.index(max(values.shape))
    spots = []
    for shift in (0, 1):
        where = [jax.random.randint(jax.random.fold_in(rng, axis), (), 0, length) for axis, length in enumerate(values.shape)]
        where[longest] = (where[longest] + shift) % values.shape[longest]
        spots.append(tuple(where))
    return values.at[spots[0]].set(least).at[spots[1]].set(largest)


def shard_levels(own_key, dims, shards, low, top_value):
    loudness = 1.0
    for axis_at, shards_of in shards:
        heights = jax.random.uniform(jax.random.fold_in(jax.random.fold_in(own_key, 6), axis_at), (shards_of,), jnp.float32, low / len(shards), top_value / len(shards))
        loudness = loudness * jnp.repeat(jnp.exp(heights), dims[axis_at] // shards_of).reshape((-1,) + (1,) * (len(dims) - 1 - axis_at))
    return loudness


def centred(own_key, shape, spread, most, cuts=(), kind=jnp.bfloat16):
    values = spread * jax.random.normal(own_key, shape, jnp.float32)
    if cuts:
        values = values * shard_levels(own_key, shape, cuts, -0.22, 0.18)
    return jnp.clip(values, -most, most).astype(kind)


def setup_inputs(seed: int = 0, part: int = 0) -> dict:
    seeds = jax.random.split(jax.random.key(seed), 6)
    part_splits = jax.random.split(jax.random.fold_in(seeds[5], part), 6)
    users = centred(part_splits[0], (NU, K), 0.21, 1.3, ((0, 16),), jnp.float32)
    items = centred(part_splits[1], (NI, K), 0.21, 1.296875, ((0, 16),))
    tile_blocks = draw_tile_blocks(jax.random.fold_in(jax.random.fold_in(seeds[5], part), 71), part)
    tile_count = draw_tile_count(jax.random.fold_in(jax.random.fold_in(seeds[5], part), 71), part)
    labels = plant((jax.random.randint(part_splits[4], (NU, SLOTS * ITEM_DEV), 0, 4) < 1).astype(jnp.int32), jax.random.fold_in(part_splits[4], 1), 0, 1)
    return {"users": users, "items": items, "tile_blocks": tile_blocks, "tile_count": tile_count, "labels": labels}


def reference(users, items, tile_blocks, tile_count, labels):
    item_groups = items.astype(jnp.float32).reshape(N_LOOP, ITEM_DEV, K)
    user_groups = users.reshape(N_LOOP, USR_DEV, K)
    label_groups = labels.reshape(N_LOOP, USR_DEV, SLOTS, ITEM_DEV)

    def block_gradient(packed_args):
        user_rows, block_list, live_count, label_tile = packed_args

        def slot_step(running, slot_index):

            def work(current):
                item_block = item_groups[block_list[slot_index]]
                scores = jnp.dot(user_rows, item_block.T, precision=lax.Precision.HIGHEST, preferred_element_type=jnp.float32)
                target = label_tile[:, slot_index, :].astype(jnp.float32)
                residual = jax.nn.sigmoid(scores) - target
                return current + jnp.dot(residual, item_block, precision=lax.Precision.HIGHEST, preferred_element_type=jnp.float32)
            return (lax.cond(slot_index < live_count, work, lambda current: current, running), None)
        start_grad = jnp.zeros((USR_DEV, K), jnp.float32)
        result, _ = lax.scan(slot_step, start_grad, jnp.arange(SLOTS, dtype=jnp.int32))
        return result
    gradient = lax.map(block_gradient, (user_groups, tile_blocks, tile_count, label_groups)).reshape(NU, K)
    grad_rms = jnp.sqrt(jnp.sum(gradient * gradient) / (NU * K) + 1e-06)
    step_scale = 0.5 / grad_rms
    return users - step_scale * gradient
```

```python
import functools

import jax
import jax.numpy as jnp
from jax import lax
from jax.experimental import pallas as pl
from jax.experimental.pallas import tpu as pltpu
from jax.sharding import PartitionSpec as P

MESH = pl.DeviceIdType.MESH


def grid_of(chips):
    inner = 1
    while (2 * inner) * (2 * inner) <= chips:
        inner *= 2
    return chips // inner, inner


def chip_at(pos, outer, inner):
    wide = inner - 1
    back = lax.div(pos, outer * wide)
    row = lax.div(pos, wide)
    step = lax.rem(pos, wide)
    odd = lax.rem(row, 2)
    column = 1 + step + odd * (wide - 1 - 2 * step)
    there = row * inner + column
    home = (outer - 1 - (pos - outer * wide)) * inner
    return back * home + (1 - back) * there


def place_of(chip, outer, inner):
    wide = inner - 1
    row = lax.div(chip, inner)
    column = lax.rem(chip, inner)
    there = lax.div(column + wide, inner)
    odd = lax.rem(row, 2)
    out = row * wide + column - 1 + odd * (wide + 1 - 2 * column)
    home = outer * wide + outer - 1 - row
    return there * out + (1 - there) * home


def kernel(n, chunks, users_hbm, items_hbm, blocks_ref, count_ref, labels_hbm, grad_hbm, scale_ref,
           users, labels, held, split, grad, mine, parts,
           load_sem, label_sem, ring_send, ring_recv, pair_send, pair_recv, own_sem, sum_sem, store_sem):
    chips = n // 2
    half = chips // 2
    outer, inner = grid_of(chips)
    depth = items_hbm.shape[0]
    height = users_hbm.shape[0]
    slots = blocks_ref.shape[1]
    piece = depth // chunks
    me = lax.axis_index("loop")
    core = lax.rem(me, 2)
    partner = me + 1 - 2 * core
    pos = place_of(lax.div(me, 2), outer, inner)

    def chip_near(offset):
        return chip_at(lax.rem(pos + offset + chips, chips), outer, inner)

    ahead = chip_near(1) * 2 + core
    behind = chip_near(-1) * 2 + core

    def rows_of(block, j):
        return pl.ds(pl.multiple_of(block * depth + j * piece, piece), piece)

    own_rows = pl.ds(pl.multiple_of(me * depth, depth), depth)
    load_items = pltpu.make_async_copy(items_hbm, held.at[own_rows], load_sem.at[0])
    load_users = pltpu.make_async_copy(users_hbm, users, load_sem.at[1])

    def load_labels(s):
        columns = pl.ds(pl.multiple_of(s * depth, depth), depth)
        return pltpu.make_async_copy(labels_hbm.at[:, columns], labels.at[s], label_sem.at[s])

    load_items.start()
    load_users.start()
    for s in range(slots):
        load_labels(s).start()

    barrier = pltpu.get_barrier_semaphore()
    for other in (ahead, behind, partner):
        pl.semaphore_signal(barrier, inc=1, device_id={"loop": other}, device_id_type=MESH)
    pl.semaphore_wait(barrier, 3)
    load_items.wait()

    def chip_of(d, s):
        return chip_near(s * (2 * d - 1))

    def ring_copy(d, hop, j, source):
        block = chip_of(d, source) * 2 + core
        spot = held.at[rows_of(block, j)]
        return pltpu.make_async_remote_copy(
            src_ref=spot, dst_ref=spot,
            send_sem=ring_send.at[d, hop - 1, j], recv_sem=ring_recv.at[d, hop - 1, j],
            device_id={"loop": behind if d else ahead}, device_id_type=MESH)

    def pair_copy(d, s, j, whose):
        block = chip_of(d, s) * 2 + whose
        spot = held.at[rows_of(block, j)]
        return pltpu.make_async_remote_copy(
            src_ref=spot, dst_ref=spot,
            send_sem=pair_send.at[d, s - 1, j], recv_sem=pair_recv.at[d, s - 1, j],
            device_id={"loop": partner}, device_id_type=MESH)

    def own_copy(whose):
        spot = held.at[pl.ds(pl.multiple_of(whose * depth, depth), depth)]
        return pltpu.make_async_remote_copy(
            src_ref=spot, dst_ref=spot, send_sem=own_sem.at[0], recv_sem=own_sem.at[1],
            device_id={"loop": partner}, device_id_type=MESH)

    def shared(d):
        return range(chunks // 2) if d == 0 else range(chunks // 2, chunks)

    order = [(d, j if d == 0 else chunks - 1 - j) for j in range(chunks) for d in (0, 1)]
    last = [(d, j) for d, j in order if j in shared(d)]

    for d, j in order:
        ring_copy(d, 1, j, 0).start()
    own_copy(me).start()

    load_users.wait()
    high = users[...].astype(jnp.bfloat16)
    split[0:height] = high
    split[height:] = (users[...] - high.astype(jnp.float32)).astype(jnp.bfloat16)
    for s in range(slots):
        load_labels(s).wait()
    count = count_ref[0]

    def slot_of(block):
        found = jnp.int32(0)
        for s in range(slots):
            gap = blocks_ref[0, s] - block
            hit = 1 - lax.min(gap * gap, jnp.int32(1))
            used = lax.min(lax.max(count - s, jnp.int32(0)), jnp.int32(1))
            found = found + hit * used * (s + 1)
        return found

    def target_of(block):
        found = slot_of(block)
        slot = lax.max(found - 1, jnp.int32(0))
        live = lax.min(found, jnp.int32(1)).astype(jnp.float32)
        label = labels[slot].astype(jnp.float32)
        return label, live

    def compute(chip, first=False):
        item = held[pl.ds(pl.multiple_of(chip * 2 * depth, 2 * depth), 2 * depth), :]
        both = lax.dot_general(split[...], item, (((1,), (1,)), ((), ())),
                               preferred_element_type=jnp.float32)
        scores = both[:height] + both[height:]
        guess = 0.5 + 0.5 * jnp.tanh(0.5 * scores)
        label0, live0 = target_of(chip * 2)
        label1, live1 = target_of(chip * 2 + 1)
        residual = jnp.concatenate(
            [(guess[:, :depth] - label0) * live0, (guess[:, depth:] - label1) * live1], axis=1)
        top = residual.astype(jnp.bfloat16)
        rest = (residual - top.astype(jnp.float32)).astype(jnp.bfloat16)
        term = (jnp.dot(top, item, preferred_element_type=jnp.float32)
                + jnp.dot(rest, item, preferred_element_type=jnp.float32))
        grad[...] = term if first else grad[...] + term

    def take_pair(d, s, js):
        for j in js:
            pair_copy(d, s, j, 1 - core).wait_recv()

    def arrive(s, d, j, onward):
        ring_copy(d, s, j, s).wait_recv()
        if onward:
            ring_copy(d, s + 1, j, s).start()
        pair_copy(d, s, j, core).start()

    def own_pair():
        own_copy(partner).wait_recv()
        compute(lax.div(me, 2), first=True)

    def earlier(s, d):
        take_pair(d, s, range(chunks))
        compute(chip_of(d, s))

    def full_step(s, final, start):
        for i, (d, j) in enumerate(order):
            arrive(s, d, j, (d, j) in last if final else True)
            if start:
                if i == len(order) // 2 - 1:
                    own_pair()
            else:
                if i == len(order) // 2 - 1:
                    earlier(s - 1, 0)
                if i == len(order) - 1:
                    earlier(s - 1, 1)

    full_step(1, half == 2, True)
    if half <= 4:
        for s in range(2, half - 1):
            full_step(s, False, False)
    else:
        lax.fori_loop(2, half - 1, lambda s, c: (full_step(s, False, False), c)[1], 0)
    if half > 2:
        full_step(half - 1, True, False)
    for d, j in last:
        arrive(half, d, j, False)
    earlier(half - 1, 0)
    earlier(half - 1, 1)
    for d in (0, 1):
        take_pair(d, half, shared(d))
    compute(chip_of(0, half))

    squares = grad[...] * grad[...]
    lanes = 128
    total = squares[:, 0:lanes]
    for k in range(1, squares.shape[1] // lanes):
        total = total + squares[:, k * lanes:(k + 1) * lanes]
    total = jnp.sum(total.reshape(height // 8, 8, lanes), axis=0)
    mine[...] = total

    def sum_copy(k):
        return pltpu.make_async_remote_copy(
            src_ref=mine, dst_ref=parts.at[n - 1 - k], send_sem=sum_sem.at[0], recv_sem=sum_sem.at[1],
            device_id={"loop": lax.rem(me + k, n)}, device_id_type=MESH)

    if n <= 16:
        for k in range(1, n):
            sum_copy(k).start()
    else:
        lax.fori_loop(1, n, lambda k, c: (sum_copy(k).start(), c)[1], 0)
    store = pltpu.make_async_copy(grad, grad_hbm, store_sem)
    store.start()

    own_copy(me).wait_send()

    def drain(s, pairs, ring):
        for d, j in pairs:
            pair_copy(d, s, j, core).wait_send()
        for d, j in ring:
            ring_copy(d, s, j, s - 1).wait_send()

    if half <= 4:
        for s in range(1, half):
            drain(s, order, order)
    else:
        lax.fori_loop(1, half, lambda s, c: (drain(s, order, order), c)[1], 0)
    drain(half, last, last)
    store.wait()

    pltpu.make_async_copy(parts, parts, sum_sem.at[1]).wait()
    pltpu.make_async_copy(parts, parts, sum_sem.at[0]).wait()
    whole = total + jnp.sum(parts[...], axis=0)
    whole = jnp.sum(jnp.sum(whole, axis=1, keepdims=True), axis=0, keepdims=True)
    entries = height * n * users_hbm.shape[1]
    rms = jnp.sqrt(whole / entries + 1e-06)
    scale_ref[...] = jnp.broadcast_to(0.5 / rms, scale_ref.shape)


def solution(mesh):
    n = mesh.shape["loop"]

    def local(users, items, tile_blocks, tile_count, labels):
        height, width = users.shape
        depth = items.shape[0]
        half = n // 4
        chunks = 4 if half <= 4 else 2
        dma = pltpu.SemaphoreType.DMA
        anywhere = pl.BlockSpec(memory_space=pl.ANY)
        scalars = pl.BlockSpec(memory_space=pltpu.SMEM)
        gradient, scale = pl.pallas_call(
            functools.partial(kernel, n, chunks),
            out_shape=(jax.ShapeDtypeStruct((height, width), jnp.float32),
                       jax.ShapeDtypeStruct((8, 128), jnp.float32)),
            in_specs=[anywhere, anywhere, scalars, scalars, anywhere],
            out_specs=(anywhere, pl.BlockSpec(memory_space=pltpu.VMEM)),
            scratch_shapes=[
                pltpu.VMEM((height, width), jnp.float32),
                pltpu.VMEM((tile_blocks.shape[1], height, depth), jnp.int32),
                pltpu.VMEM((n * depth, width), jnp.bfloat16),
                pltpu.VMEM((2 * height, width), jnp.bfloat16),
                pltpu.VMEM((height, width), jnp.float32),
                pltpu.VMEM((8, 128), jnp.float32),
                pltpu.VMEM((n - 1, 8, 128), jnp.float32),
                dma((2,)),
                dma((tile_blocks.shape[1],)),
                dma((2, half, chunks)),
                dma((2, half, chunks)),
                dma((2, half, chunks)),
                dma((2, half, chunks)),
                dma((2,)),
                dma((2,)),
                dma(()),
            ],
            compiler_params=pltpu.CompilerParams(
                collective_id=0, has_side_effects=True, vmem_limit_bytes=60 * 1024 * 1024),
            name="gather_gradient",
        )(users, items, tile_blocks, tile_count, labels)
        return users - scale[0, 0] * gradient

    rows = P(("group", "loop"), None)
    return jax.shard_map(local, mesh=mesh, in_specs=(rows, rows, rows, P(("group", "loop")), rows),
                         out_specs=rows, check_vma=False)
```

```python
import functools

import jax
import jax.numpy as jnp
from jax import lax
from jax.experimental import pallas as pl
from jax.experimental.pallas import tpu as pltpu
from jax.sharding import PartitionSpec as P

MESH = pl.DeviceIdType.MESH


def grid_of(chips):
    inner = 1
    while (2 * inner) * (2 * inner) <= chips:
        inner *= 2
    return chips // inner, inner


def chip_at(pos, outer, inner):
    wide = inner - 1
    back = lax.div(pos, outer * wide)
    row = lax.div(pos, wide)
    step = lax.rem(pos, wide)
    odd = lax.rem(row, 2)
    column = 1 + step + odd * (wide - 1 - 2 * step)
    there = row * inner + column
    home = (outer - 1 - (pos - outer * wide)) * inner
    return back * home + (1 - back) * there


def place_of(chip, outer, inner):
    wide = inner - 1
    row = lax.div(chip, inner)
    column = lax.rem(chip, inner)
    there = lax.div(column + wide, inner)
    odd = lax.rem(row, 2)
    out = row * wide + column - 1 + odd * (wide + 1 - 2 * column)
    home = outer * wide + outer - 1 - row
    return there * out + (1 - there) * home


def kernel(n, chunks, users_hbm, items_hbm, blocks_ref, count_ref, labels_hbm, grad_hbm, scale_ref,
           users, labels, held, split, grad, mine, parts,
           load_sem, label_sem, ring_send, ring_recv, pair_send, pair_recv, own_sem, sum_sem, store_sem):
    chips = n // 2
    half = chips // 2
    outer, inner = grid_of(chips)
    depth = items_hbm.shape[0]
    height = users_hbm.shape[0]
    slots = blocks_ref.shape[1]
    piece = depth // chunks
    me = lax.axis_index("loop")
    core = lax.rem(me, 2)
    partner = me + 1 - 2 * core
    pos = place_of(lax.div(me, 2), outer, inner)

    def chip_near(offset):
        return chip_at(lax.rem(pos + offset + chips, chips), outer, inner)

    ahead = chip_near(1) * 2 + core
    behind = chip_near(-1) * 2 + core

    def rows_of(block, j):
        return pl.ds(pl.multiple_of(block * depth + j * piece, piece), piece)

    own_rows = pl.ds(pl.multiple_of(me * depth, depth), depth)
    load_items = pltpu.make_async_copy(items_hbm, held.at[own_rows], load_sem.at[0])
    load_users = pltpu.make_async_copy(users_hbm, users, load_sem.at[1])

    def load_labels(s):
        columns = pl.ds(pl.multiple_of(s * depth, depth), depth)
        return pltpu.make_async_copy(labels_hbm.at[:, columns], labels.at[s], label_sem.at[s])

    load_items.start()
    load_users.start()
    for s in range(slots):
        load_labels(s).start()

    barrier = pltpu.get_barrier_semaphore()
    for other in (ahead, behind, partner):
        pl.semaphore_signal(barrier, inc=1, device_id={"loop": other}, device_id_type=MESH)
    pl.semaphore_wait(barrier, 3)
    load_items.wait()

    known = {}

    def chip_of(d, s):
        if not isinstance(s, int):
            return chip_near(s * (2 * d - 1))
        if (d, s) not in known:
            known[d, s] = chip_near(s * (2 * d - 1))
        return known[d, s]

    for s in {0, 1, 2, half - 2, half - 1, half} | (set(range(half)) if half <= 4 else set()):
        for d in (0, 1):
            chip_of(d, s)

    def ring_copy(d, hop, j, source):
        block = chip_of(d, source) * 2 + core
        spot = held.at[rows_of(block, j)]
        return pltpu.make_async_remote_copy(
            src_ref=spot, dst_ref=spot,
            send_sem=ring_send.at[d, hop - 1, j], recv_sem=ring_recv.at[d, hop - 1, j],
            device_id={"loop": behind if d else ahead}, device_id_type=MESH)

    def pair_copy(d, s, j, whose):
        block = chip_of(d, s) * 2 + whose
        spot = held.at[rows_of(block, j)]
        return pltpu.make_async_remote_copy(
            src_ref=spot, dst_ref=spot,
            send_sem=pair_send.at[d, s - 1, j], recv_sem=pair_recv.at[d, s - 1, j],
            device_id={"loop": partner}, device_id_type=MESH)

    def own_copy(whose):
        spot = held.at[pl.ds(pl.multiple_of(whose * depth, depth), depth)]
        return pltpu.make_async_remote_copy(
            src_ref=spot, dst_ref=spot, send_sem=own_sem.at[0], recv_sem=own_sem.at[1],
            device_id={"loop": partner}, device_id_type=MESH)

    def shared(d):
        return range(chunks // 2) if d == 0 else range(chunks // 2, chunks)

    order = [(d, j if d == 0 else chunks - 1 - j) for j in range(chunks) for d in (0, 1)]
    last = [(d, j) for d, j in order if j in shared(d)]

    for d, j in order:
        ring_copy(d, 1, j, 0).start()
    own_copy(me).start()

    load_users.wait()
    high = users[...].astype(jnp.bfloat16)
    split[0:height] = high
    split[height:] = (users[...] - high.astype(jnp.float32)).astype(jnp.bfloat16)
    for s in range(slots):
        load_labels(s).wait()
    count = count_ref[0]

    def slot_of(block):
        found = jnp.int32(0)
        for s in range(slots):
            gap = blocks_ref[0, s] - block
            hit = 1 - lax.min(gap * gap, jnp.int32(1))
            used = lax.min(lax.max(count - s, jnp.int32(0)), jnp.int32(1))
            found = found + hit * used * (s + 1)
        return found

    def target_of(block):
        found = slot_of(block)
        slot = lax.max(found - 1, jnp.int32(0))
        live = lax.min(found, jnp.int32(1)).astype(jnp.float32)
        label = labels[slot].astype(jnp.float32)
        return label, live

    def compute(chip, first=False):
        item = held[pl.ds(pl.multiple_of(chip * 2 * depth, 2 * depth), 2 * depth), :]
        both = lax.dot_general(split[...], item, (((1,), (1,)), ((), ())),
                               preferred_element_type=jnp.float32)
        scores = both[:height] + both[height:]
        guess = 0.5 + 0.5 * jnp.tanh(0.5 * scores)
        label0, live0 = target_of(chip * 2)
        label1, live1 = target_of(chip * 2 + 1)
        residual = jnp.concatenate(
            [(guess[:, :depth] - label0) * live0, (guess[:, depth:] - label1) * live1], axis=1)
        top = residual.astype(jnp.bfloat16)
        rest = (residual - top.astype(jnp.float32)).astype(jnp.bfloat16)
        term = (jnp.dot(top, item, preferred_element_type=jnp.float32)
                + jnp.dot(rest, item, preferred_element_type=jnp.float32))
        grad[...] = term if first else grad[...] + term

    def take_pair(d, s, js):
        for j in js:
            pair_copy(d, s, j, 1 - core).wait_recv()

    def arrive(s, d, j, onward):
        ring_copy(d, s, j, s).wait_recv()
        if onward:
            ring_copy(d, s + 1, j, s).start()
        pair_copy(d, s, j, core).start()

    def own_pair():
        own_copy(partner).wait_recv()
        compute(lax.div(me, 2), first=True)

    def earlier(s, d):
        take_pair(d, s, range(chunks))
        compute(chip_of(d, s))

    def full_step(s, final, start):
        for i, (d, j) in enumerate(order):
            arrive(s, d, j, (d, j) in last if final else True)
            if start:
                if i == len(order) // 2 - 1:
                    own_pair()
            else:
                if i == len(order) // 2 - 1:
                    earlier(s - 1, 0)
                if i == len(order) - 1:
                    earlier(s - 1, 1)

    full_step(1, half == 2, True)
    if half <= 4:
        for s in range(2, half - 1):
            full_step(s, False, False)
    else:
        lax.fori_loop(2, half - 1, lambda s, c: (full_step(s, False, False), c)[1], 0)
    if half > 2:
        full_step(half - 1, True, False)
    earlier(half - 1, 0)
    for i, (d, j) in enumerate(last):
        arrive(half, d, j, False)
        if i == len(last) // 2 - 1:
            earlier(half - 1, 1)
    for d in (0, 1):
        take_pair(d, half, shared(d))
    compute(chip_of(0, half))

    squares = grad[...] * grad[...]
    lanes = 128
    total = squares[:, 0:lanes]
    for k in range(1, squares.shape[1] // lanes):
        total = total + squares[:, k * lanes:(k + 1) * lanes]
    total = jnp.sum(total.reshape(height // 8, 8, lanes), axis=0)
    mine[...] = total

    def sum_copy(k):
        return pltpu.make_async_remote_copy(
            src_ref=mine, dst_ref=parts.at[n - 1 - k], send_sem=sum_sem.at[0], recv_sem=sum_sem.at[1],
            device_id={"loop": lax.rem(me + k, n)}, device_id_type=MESH)

    if n <= 16:
        for k in range(1, n):
            sum_copy(k).start()
    else:
        lax.fori_loop(1, n, lambda k, c: (sum_copy(k).start(), c)[1], 0)
    store = pltpu.make_async_copy(grad, grad_hbm, store_sem)
    store.start()

    own_copy(me).wait_send()

    def drain(s, pairs, ring):
        for d, j in pairs:
            pair_copy(d, s, j, core).wait_send()
        for d, j in ring:
            ring_copy(d, s, j, s - 1).wait_send()

    if half <= 4:
        for s in range(1, half):
            drain(s, order, order)
    else:
        lax.fori_loop(1, half, lambda s, c: (drain(s, order, order), c)[1], 0)
    drain(half, last, last)
    store.wait()

    pltpu.make_async_copy(parts, parts, sum_sem.at[1]).wait()
    pltpu.make_async_copy(parts, parts, sum_sem.at[0]).wait()
    whole = total + jnp.sum(parts[...], axis=0)
    whole = jnp.sum(jnp.sum(whole, axis=1, keepdims=True), axis=0, keepdims=True)
    entries = height * n * users_hbm.shape[1]
    rms = jnp.sqrt(whole / entries + 1e-06)
    scale_ref[...] = 0.5 / rms


def solution(mesh):
    n = mesh.shape["loop"]

    def local(users, items, tile_blocks, tile_count, labels):
        height, width = users.shape
        depth = items.shape[0]
        half = n // 4
        chunks = 4 if half <= 4 else 2
        dma = pltpu.SemaphoreType.DMA
        scratch = 4 * height * (3 * width + labels.shape[1]) + 2 * n * depth * width
        grant = 58 * 1024 * 1024
        anywhere = pl.BlockSpec(memory_space=pl.ANY)
        far = pl.BlockSpec(memory_space=pltpu.HBM)
        scalars = pl.BlockSpec(memory_space=pltpu.SMEM)
        gradient, scale = pl.pallas_call(
            functools.partial(kernel, n, chunks),
            out_shape=(jax.ShapeDtypeStruct((height, width), jnp.float32),
                       jax.ShapeDtypeStruct((1, 1), jnp.float32)),
            in_specs=[far, far, scalars, scalars, far],
            out_specs=(anywhere, pl.BlockSpec(memory_space=pltpu.VMEM)),
            scratch_shapes=[
                pltpu.VMEM((height, width), jnp.float32),
                pltpu.VMEM((tile_blocks.shape[1], height, depth), jnp.int32),
                pltpu.VMEM((n * depth, width), jnp.bfloat16),
                pltpu.VMEM((2 * height, width), jnp.bfloat16),
                pltpu.VMEM((height, width), jnp.float32),
                pltpu.VMEM((8, 128), jnp.float32),
                pltpu.VMEM((n - 1, 8, 128), jnp.float32),
                dma((2,)),
                dma((tile_blocks.shape[1],)),
                dma((2, half, chunks)),
                dma((2, half, chunks)),
                dma((2, half, chunks)),
                dma((2, half, chunks)),
                dma((2,)),
                dma((2,)),
                dma(()),
            ],
            compiler_params=pltpu.CompilerParams(
                collective_id=0, has_side_effects=True, vmem_limit_bytes=grant),
            name="gather_gradient",
        )(users, items, tile_blocks, tile_count, labels)
        return users - scale[0, 0] * gradient

    rows = P(("group", "loop"), None)
    return jax.shard_map(local, mesh=mesh, in_specs=(rows, rows, rows, P(("group", "loop")), rows),
                         out_specs=rows, check_vma=False)
```

```python
import functools

import jax
import jax.numpy as jnp
from jax import lax
from jax.experimental import pallas as pl
from jax.experimental.pallas import tpu as pltpu
from jax.sharding import PartitionSpec as P

MESH = pl.DeviceIdType.MESH


def grid_of(chips):
    inner = 1
    while (2 * inner) * (2 * inner) <= chips:
        inner *= 2
    return chips // inner, inner


def chip_at(pos, outer, inner):
    wide = inner - 1
    back = lax.div(pos, outer * wide)
    row = lax.div(pos, wide)
    step = lax.rem(pos, wide)
    odd = lax.rem(row, 2)
    column = 1 + step + odd * (wide - 1 - 2 * step)
    there = row * inner + column
    home = (outer - 1 - (pos - outer * wide)) * inner
    return back * home + (1 - back) * there


def place_of(chip, outer, inner):
    wide = inner - 1
    row = lax.div(chip, inner)
    column = lax.rem(chip, inner)
    there = lax.div(column + wide, inner)
    odd = lax.rem(row, 2)
    out = row * wide + column - 1 + odd * (wide + 1 - 2 * column)
    home = outer * wide + outer - 1 - row
    return there * out + (1 - there) * home


def kernel(n, chunks, users_hbm, items_hbm, blocks_ref, count_ref, labels_hbm, grad_hbm,
           users, labels, held, split, grad, mine, parts,
           load_sem, label_sem, ring_send, ring_recv, pair_send, pair_recv, own_sem, sum_sem, store_sem):
    chips = n // 2
    half = chips // 2
    outer, inner = grid_of(chips)
    depth = items_hbm.shape[0]
    height = users_hbm.shape[0]
    slots = blocks_ref.shape[1]
    piece = depth // chunks
    me = lax.axis_index("loop")
    core = lax.rem(me, 2)
    partner = me + 1 - 2 * core
    pos = place_of(lax.div(me, 2), outer, inner)

    def chip_near(offset):
        return chip_at(lax.rem(pos + offset + chips, chips), outer, inner)

    ahead = chip_near(1) * 2 + core
    behind = chip_near(-1) * 2 + core

    def rows_of(block, j):
        return pl.ds(pl.multiple_of(block * depth + j * piece, piece), piece)

    own_rows = pl.ds(pl.multiple_of(me * depth, depth), depth)
    load_items = pltpu.make_async_copy(items_hbm, held.at[own_rows], load_sem.at[0])
    load_users = pltpu.make_async_copy(users_hbm, users, load_sem.at[1])

    def load_labels(s):
        columns = pl.ds(pl.multiple_of(s * depth, depth), depth)
        return pltpu.make_async_copy(labels_hbm.at[:, columns], labels.at[s], label_sem.at[s])

    load_items.start()
    load_users.start()
    for s in range(slots):
        load_labels(s).start()

    barrier = pltpu.get_barrier_semaphore()
    for other in (ahead, behind, partner):
        pl.semaphore_signal(barrier, inc=1, device_id={"loop": other}, device_id_type=MESH)
    pl.semaphore_wait(barrier, 3)
    load_items.wait()

    known = {}

    def chip_of(d, s):
        if not isinstance(s, int):
            return chip_near(s * (2 * d - 1))
        if (d, s) not in known:
            known[d, s] = chip_near(s * (2 * d - 1))
        return known[d, s]

    for s in {0, 1, 2, half - 2, half - 1, half} | (set(range(half)) if half <= 4 else set()):
        for d in (0, 1):
            chip_of(d, s)

    def ring_copy(d, hop, j, source):
        block = chip_of(d, source) * 2 + core
        spot = held.at[rows_of(block, j)]
        return pltpu.make_async_remote_copy(
            src_ref=spot, dst_ref=spot,
            send_sem=ring_send.at[d, hop - 1, j], recv_sem=ring_recv.at[d, hop - 1, j],
            device_id={"loop": behind if d else ahead}, device_id_type=MESH)

    def pair_copy(d, s, j, whose):
        block = chip_of(d, s) * 2 + whose
        spot = held.at[rows_of(block, j)]
        return pltpu.make_async_remote_copy(
            src_ref=spot, dst_ref=spot,
            send_sem=pair_send.at[d, s - 1, j], recv_sem=pair_recv.at[d, s - 1, j],
            device_id={"loop": partner}, device_id_type=MESH)

    def own_copy(whose):
        spot = held.at[pl.ds(pl.multiple_of(whose * depth, depth), depth)]
        return pltpu.make_async_remote_copy(
            src_ref=spot, dst_ref=spot, send_sem=own_sem.at[0], recv_sem=own_sem.at[1],
            device_id={"loop": partner}, device_id_type=MESH)

    def shared(d):
        return range(chunks // 2) if d == 0 else range(chunks // 2, chunks)

    order = [(d, j if d == 0 else chunks - 1 - j) for j in range(chunks) for d in (0, 1)]
    last = [(d, j) for d, j in order if j in shared(d)]

    for d, j in order:
        ring_copy(d, 1, j, 0).start()
    own_copy(me).start()

    load_users.wait()
    high = users[...].astype(jnp.bfloat16)
    split[0:height] = high
    split[height:] = (users[...] - high.astype(jnp.float32)).astype(jnp.bfloat16)
    for s in range(slots):
        load_labels(s).wait()
    count = count_ref[0]

    def slot_of(block):
        found = jnp.int32(0)
        for s in range(slots):
            gap = blocks_ref[0, s] - block
            hit = 1 - lax.min(gap * gap, jnp.int32(1))
            used = lax.min(lax.max(count - s, jnp.int32(0)), jnp.int32(1))
            found = found + hit * used * (s + 1)
        return found

    def target_of(block):
        found = slot_of(block)
        slot = lax.max(found - 1, jnp.int32(0))
        live = lax.min(found, jnp.int32(1)).astype(jnp.float32)
        label = labels[slot].astype(jnp.float32)
        return label, live

    def compute(chip, first=False):
        item = held[pl.ds(pl.multiple_of(chip * 2 * depth, 2 * depth), 2 * depth), :]
        both = lax.dot_general(split[...], item, (((1,), (1,)), ((), ())),
                               preferred_element_type=jnp.float32)
        scores = both[:height] + both[height:]
        guess = 0.5 + 0.5 * jnp.tanh(0.5 * scores)
        label0, live0 = target_of(chip * 2)
        label1, live1 = target_of(chip * 2 + 1)
        residual = jnp.concatenate(
            [(guess[:, :depth] - label0) * live0, (guess[:, depth:] - label1) * live1], axis=1)
        top = residual.astype(jnp.bfloat16)
        rest = (residual - top.astype(jnp.float32)).astype(jnp.bfloat16)
        term = (jnp.dot(top, item, preferred_element_type=jnp.float32)
                + jnp.dot(rest, item, preferred_element_type=jnp.float32))
        grad[...] = term if first else grad[...] + term

    def take_pair(d, s, js):
        for j in js:
            pair_copy(d, s, j, 1 - core).wait_recv()

    def arrive(s, d, j, onward):
        ring_copy(d, s, j, s).wait_recv()
        if onward:
            ring_copy(d, s + 1, j, s).start()
        pair_copy(d, s, j, core).start()

    def own_pair():
        own_copy(partner).wait_recv()
        compute(lax.div(me, 2), first=True)

    def earlier(s, d):
        take_pair(d, s, range(chunks))
        compute(chip_of(d, s))

    def full_step(s, final, start):
        for i, (d, j) in enumerate(order):
            arrive(s, d, j, (d, j) in last if final else True)
            if start:
                if i == len(order) // 2 - 1:
                    own_pair()
            else:
                if i == len(order) // 2 - 1:
                    earlier(s - 1, 0)
                if i == len(order) - 1:
                    earlier(s - 1, 1)

    full_step(1, half == 2, True)
    if half <= 4:
        for s in range(2, half - 1):
            full_step(s, False, False)
    else:
        lax.fori_loop(2, half - 1, lambda s, c: (full_step(s, False, False), c)[1], 0)
    if half > 2:
        full_step(half - 1, True, False)
    earlier(half - 1, 0)
    for i, (d, j) in enumerate(last):
        arrive(half, d, j, False)
        if i == len(last) // 2 - 1:
            earlier(half - 1, 1)
    for d in (0, 1):
        take_pair(d, half, shared(d))
    compute(chip_of(0, half))

    squares = grad[...] * grad[...]
    lanes = 128
    total = squares[:, 0:lanes]
    for k in range(1, squares.shape[1] // lanes):
        total = total + squares[:, k * lanes:(k + 1) * lanes]
    total = jnp.sum(jnp.sum(total.reshape(height // 8, 8, lanes), axis=0), axis=0, keepdims=True)
    mine[...] = total

    def sum_copy(k):
        return pltpu.make_async_remote_copy(
            src_ref=mine, dst_ref=parts.at[n - 1 - k], send_sem=sum_sem.at[0], recv_sem=sum_sem.at[1],
            device_id={"loop": lax.rem(me + k, n)}, device_id_type=MESH)

    if n <= 16:
        for k in range(1, n):
            sum_copy(k).start()
    else:
        lax.fori_loop(1, n, lambda k, c: (sum_copy(k).start(), c)[1], 0)

    own_copy(me).wait_send()

    def drain(s, pairs, ring):
        for d, j in pairs:
            pair_copy(d, s, j, core).wait_send()
        for d, j in ring:
            ring_copy(d, s, j, s - 1).wait_send()

    if half <= 4:
        for s in range(1, half):
            drain(s, order, order)
    else:
        lax.fori_loop(1, half, lambda s, c: (drain(s, order, order), c)[1], 0)
    drain(half, last, last)

    pltpu.make_async_copy(parts, parts, sum_sem.at[1]).wait()
    pltpu.make_async_copy(parts, parts, sum_sem.at[0]).wait()
    whole = total + jnp.sum(parts[...], axis=0)
    whole = jnp.sum(jnp.sum(whole, axis=1, keepdims=True), axis=0, keepdims=True)
    entries = height * n * users_hbm.shape[1]
    rms = jnp.sqrt(whole / entries + 1e-06)
    grad[...] = users[...] - (0.5 / rms) * grad[...]
    store = pltpu.make_async_copy(grad, grad_hbm, store_sem)
    store.start()
    store.wait()


def solution(mesh):
    n = mesh.shape["loop"]

    def local(users, items, tile_blocks, tile_count, labels):
        height, width = users.shape
        depth = items.shape[0]
        half = n // 4
        chunks = 4 if half <= 4 else 2
        dma = pltpu.SemaphoreType.DMA
        scratch = 4 * height * (3 * width + labels.shape[1]) + 2 * n * depth * width
        grant = 58 * 1024 * 1024
        anywhere = pl.BlockSpec(memory_space=pl.ANY)
        far = pl.BlockSpec(memory_space=pltpu.HBM)
        scalars = pl.BlockSpec(memory_space=pltpu.SMEM)
        return pl.pallas_call(
            functools.partial(kernel, n, chunks),
            out_shape=jax.ShapeDtypeStruct((height, width), jnp.float32),
            in_specs=[far, far, scalars, scalars, far],
            out_specs=anywhere,
            scratch_shapes=[
                pltpu.VMEM((height, width), jnp.float32),
                pltpu.VMEM((tile_blocks.shape[1], height, depth), jnp.int32),
                pltpu.VMEM((n * depth, width), jnp.bfloat16),
                pltpu.VMEM((2 * height, width), jnp.bfloat16),
                pltpu.VMEM((height, width), jnp.float32),
                pltpu.VMEM((1, 128), jnp.float32),
                pltpu.VMEM((n - 1, 1, 128), jnp.float32),
                dma((2,)),
                dma((tile_blocks.shape[1],)),
                dma((2, half, chunks)),
                dma((2, half, chunks)),
                dma((2, half, chunks)),
                dma((2, half, chunks)),
                dma((2,)),
                dma((2,)),
                dma(()),
            ],
            compiler_params=pltpu.CompilerParams(
                collective_id=0, has_side_effects=True, vmem_limit_bytes=grant),
            name="gather_gradient",
        )(users, items, tile_blocks, tile_count, labels)

    rows = P(("group", "loop"), None)
    return jax.shard_map(local, mesh=mesh, in_specs=(rows, rows, rows, P(("group", "loop")), rows),
                         out_specs=rows, check_vma=False)
```

```python
import functools

import jax
import jax.numpy as jnp
from jax import lax
from jax.experimental import pallas as pl
from jax.experimental.pallas import tpu as pltpu
from jax.sharding import PartitionSpec as P

MESH = pl.DeviceIdType.MESH


def grid_of(chips):
    inner = 1
    while (2 * inner) * (2 * inner) <= chips:
        inner *= 2
    return chips // inner, inner


def chip_at(pos, outer, inner):
    wide = inner - 1
    back = lax.div(pos, outer * wide)
    row = lax.div(pos, wide)
    step = lax.rem(pos, wide)
    odd = lax.rem(row, 2)
    column = 1 + step + odd * (wide - 1 - 2 * step)
    there = row * inner + column
    home = (outer - 1 - (pos - outer * wide)) * inner
    return back * home + (1 - back) * there


def place_of(chip, outer, inner):
    wide = inner - 1
    row = lax.div(chip, inner)
    column = lax.rem(chip, inner)
    there = lax.div(column + wide, inner)
    odd = lax.rem(row, 2)
    out = row * wide + column - 1 + odd * (wide + 1 - 2 * column)
    home = outer * wide + outer - 1 - row
    return there * out + (1 - there) * home


def kernel(n, chunks, users_hbm, items_hbm, blocks_ref, count_ref, labels_hbm, grad_hbm,
           users, labels, held, split, grad, mine, parts,
           load_sem, label_sem, ring_send, ring_recv, pair_send, pair_recv, own_sem, sum_sem, store_sem):
    chips = n // 2
    half = chips // 2
    outer, inner = grid_of(chips)
    depth = items_hbm.shape[0]
    height = users_hbm.shape[0]
    slots = blocks_ref.shape[1]
    piece = depth // chunks
    me = lax.axis_index("loop")
    core = lax.rem(me, 2)
    partner = me + 1 - 2 * core
    pos = place_of(lax.div(me, 2), outer, inner)

    def chip_near(offset):
        return chip_at(lax.rem(pos + offset + chips, chips), outer, inner)

    ahead = chip_near(1) * 2 + core
    behind = chip_near(-1) * 2 + core

    def rows_of(block, j):
        return pl.ds(pl.multiple_of(block * depth + j * piece, piece), piece)

    own_rows = pl.ds(pl.multiple_of(me * depth, depth), depth)
    load_items = pltpu.make_async_copy(items_hbm, held.at[own_rows], load_sem.at[0])
    load_users = pltpu.make_async_copy(users_hbm, users, load_sem.at[1])

    def load_labels(s):
        columns = pl.ds(pl.multiple_of(s * depth, depth), depth)
        return pltpu.make_async_copy(labels_hbm.at[:, columns], labels.at[s], label_sem.at[s])

    load_items.start()
    load_users.start()
    for s in range(slots):
        load_labels(s).start()

    barrier = pltpu.get_barrier_semaphore()
    for other in (ahead, behind, partner):
        pl.semaphore_signal(barrier, inc=1, device_id={"loop": other}, device_id_type=MESH)
    pl.semaphore_wait(barrier, 3)
    load_items.wait()

    known = {}

    def chip_of(d, s):
        if not isinstance(s, int):
            return chip_near(s * (2 * d - 1))
        if (d, s) not in known:
            known[d, s] = chip_near(s * (2 * d - 1))
        return known[d, s]

    for s in {0, 1, 2, half - 2, half - 1, half} | (set(range(half)) if half <= 4 else set()):
        for d in (0, 1):
            chip_of(d, s)

    def ring_copy(d, hop, j, source):
        block = chip_of(d, source) * 2 + core
        spot = held.at[rows_of(block, j)]
        return pltpu.make_async_remote_copy(
            src_ref=spot, dst_ref=spot,
            send_sem=ring_send.at[d, hop - 1, j], recv_sem=ring_recv.at[d, hop - 1, j],
            device_id={"loop": behind if d else ahead}, device_id_type=MESH)

    def pair_copy(d, s, j, whose):
        block = chip_of(d, s) * 2 + whose
        spot = held.at[rows_of(block, j)]
        return pltpu.make_async_remote_copy(
            src_ref=spot, dst_ref=spot,
            send_sem=pair_send.at[d, s - 1, j], recv_sem=pair_recv.at[d, s - 1, j],
            device_id={"loop": partner}, device_id_type=MESH)

    def own_copy(whose):
        spot = held.at[pl.ds(pl.multiple_of(whose * depth, depth), depth)]
        return pltpu.make_async_remote_copy(
            src_ref=spot, dst_ref=spot, send_sem=own_sem.at[0], recv_sem=own_sem.at[1],
            device_id={"loop": partner}, device_id_type=MESH)

    def shared(d):
        return range(chunks // 2) if d == 0 else range(chunks // 2, chunks)

    order = [(d, j if d == 0 else chunks - 1 - j) for j in range(chunks) for d in (0, 1)]
    last = [(d, j) for d, j in order if j in shared(d)]

    for d, j in order:
        ring_copy(d, 1, j, 0).start()
    own_copy(me).start()

    load_users.wait()
    high = users[...].astype(jnp.bfloat16)
    split[0:height] = high
    split[height:] = (users[...] - high.astype(jnp.float32)).astype(jnp.bfloat16)
    for s in range(slots):
        load_labels(s).wait()
    count = count_ref[0]

    def slot_of(block):
        found = jnp.int32(0)
        for s in range(slots):
            gap = blocks_ref[0, s] - block
            hit = 1 - lax.min(gap * gap, jnp.int32(1))
            used = lax.min(lax.max(count - s, jnp.int32(0)), jnp.int32(1))
            found = found + hit * used * (s + 1)
        return found

    def target_of(block):
        found = slot_of(block)
        slot = lax.max(found - 1, jnp.int32(0))
        live = lax.min(found, jnp.int32(1)).astype(jnp.float32)
        label = labels[slot].astype(jnp.float32)
        return label, live

    def compute(chip, first=False):
        item = held[pl.ds(pl.multiple_of(chip * 2 * depth, 2 * depth), 2 * depth), :]
        both = lax.dot_general(split[...], item, (((1,), (1,)), ((), ())),
                               preferred_element_type=jnp.float32)
        scores = both[:height] + both[height:]
        guess = 0.5 + 0.5 * jnp.tanh(0.5 * scores)
        label0, live0 = target_of(chip * 2)
        label1, live1 = target_of(chip * 2 + 1)
        residual = jnp.concatenate(
            [(guess[:, :depth] - label0) * live0, (guess[:, depth:] - label1) * live1], axis=1)
        top = residual.astype(jnp.bfloat16)
        rest = (residual - top.astype(jnp.float32)).astype(jnp.bfloat16)
        term = (jnp.dot(top, item, preferred_element_type=jnp.float32)
                + jnp.dot(rest, item, preferred_element_type=jnp.float32))
        grad[...] = term if first else grad[...] + term

    def take_pair(d, s, js):
        for j in js:
            pair_copy(d, s, j, 1 - core).wait_recv()

    def arrive(s, d, j, onward):
        ring_copy(d, s, j, s).wait_recv()
        if onward:
            ring_copy(d, s + 1, j, s).start()
        pair_copy(d, s, j, core).start()

    def own_pair():
        own_copy(partner).wait_recv()
        compute(lax.div(me, 2), first=True)

    def earlier(s, d):
        take_pair(d, s, range(chunks))
        compute(chip_of(d, s))

    def full_step(s, final, start):
        for i, (d, j) in enumerate(order):
            arrive(s, d, j, (d, j) in last if final else True)
            if start:
                if i == len(order) // 2 - 1:
                    own_pair()
            else:
                if i == len(order) // 2 - 1:
                    earlier(s - 1, 0)
                if i == len(order) - 1:
                    earlier(s - 1, 1)

    full_step(1, half == 2, True)
    if half <= 4:
        for s in range(2, half - 1):
            full_step(s, False, False)
    else:
        lax.fori_loop(2, half - 1, lambda s, c: (full_step(s, False, False), c)[1], 0)
    if half > 2:
        full_step(half - 1, True, False)
    for i, (d, j) in enumerate(last):
        arrive(half, d, j, False)
        if i == len(last) // 2 - 1:
            earlier(half - 1, 0)
    earlier(half - 1, 1)
    for d in (0, 1):
        take_pair(d, half, shared(d))
    compute(chip_of(0, half))

    squares = grad[...] * grad[...]
    lanes = 128
    total = squares[:, 0:lanes]
    for k in range(1, squares.shape[1] // lanes):
        total = total + squares[:, k * lanes:(k + 1) * lanes]
    total = jnp.sum(jnp.sum(total.reshape(height // 8, 8, lanes), axis=0), axis=0, keepdims=True)
    mine[...] = total

    def sum_copy(k):
        return pltpu.make_async_remote_copy(
            src_ref=mine, dst_ref=parts.at[n - 1 - k], send_sem=sum_sem.at[0], recv_sem=sum_sem.at[1],
            device_id={"loop": lax.rem(me + k, n)}, device_id_type=MESH)

    if n <= 16:
        for k in range(1, n):
            sum_copy(k).start()
    else:
        lax.fori_loop(1, n, lambda k, c: (sum_copy(k).start(), c)[1], 0)

    own_copy(me).wait_send()

    def drain(s, pairs, ring):
        for d, j in pairs:
            pair_copy(d, s, j, core).wait_send()
        for d, j in ring:
            ring_copy(d, s, j, s - 1).wait_send()

    if half <= 4:
        for s in range(1, half):
            drain(s, order, order)
    else:
        lax.fori_loop(1, half, lambda s, c: (drain(s, order, order), c)[1], 0)
    drain(half, last, last)

    pltpu.make_async_copy(parts, parts, sum_sem.at[1]).wait()
    pltpu.make_async_copy(parts, parts, sum_sem.at[0]).wait()
    whole = total + jnp.sum(parts[...], axis=0)
    whole = jnp.sum(jnp.sum(whole, axis=1, keepdims=True), axis=0, keepdims=True)
    entries = height * n * users_hbm.shape[1]
    rms = jnp.sqrt(whole / entries + 1e-06)
    grad[...] = users[...] - (0.5 / rms) * grad[...]
    store = pltpu.make_async_copy(grad, grad_hbm, store_sem)
    store.start()
    store.wait()


def solution(mesh):
    n = mesh.shape["loop"]

    def local(users, items, tile_blocks, tile_count, labels):
        height, width = users.shape
        depth = items.shape[0]
        half = n // 4
        chunks = 4 if half <= 4 else 2
        dma = pltpu.SemaphoreType.DMA
        scratch = 4 * height * (3 * width + labels.shape[1]) + 2 * n * depth * width
        grant = 58 * 1024 * 1024
        anywhere = pl.BlockSpec(memory_space=pl.ANY)
        far = pl.BlockSpec(memory_space=pltpu.HBM)
        scalars = pl.BlockSpec(memory_space=pltpu.SMEM)
        return pl.pallas_call(
            functools.partial(kernel, n, chunks),
            out_shape=jax.ShapeDtypeStruct((height, width), jnp.float32),
            in_specs=[far, far, scalars, scalars, far],
            out_specs=anywhere,
            scratch_shapes=[
                pltpu.VMEM((height, width), jnp.float32),
                pltpu.VMEM((tile_blocks.shape[1], height, depth), jnp.int32),
                pltpu.VMEM((n * depth, width), jnp.bfloat16),
                pltpu.VMEM((2 * height, width), jnp.bfloat16),
                pltpu.VMEM((height, width), jnp.float32),
                pltpu.VMEM((1, 128), jnp.float32),
                pltpu.VMEM((n - 1, 1, 128), jnp.float32),
                dma((2,)),
                dma((tile_blocks.shape[1],)),
                dma((2, half, chunks)),
                dma((2, half, chunks)),
                dma((2, half, chunks)),
                dma((2, half, chunks)),
                dma((2,)),
                dma((2,)),
                dma(()),
            ],
            compiler_params=pltpu.CompilerParams(
                collective_id=0, has_side_effects=True, vmem_limit_bytes=grant),
            name="gather_gradient",
        )(users, items, tile_blocks, tile_count, labels)

    rows = P(("group", "loop"), None)
    return jax.shard_map(local, mesh=mesh, in_specs=(rows, rows, rows, P(("group", "loop")), rows),
                         out_specs=rows, check_vma=False)
```
